32 devices in a mesh: slab: 4 (over x, core), trace: 8 (over z, y).
Axes of the slice: x: 2, y: 2, z: 4, core: 2. Of those that a mesh axis runs over, the one named last changes fastest.
Arguments:
- incident: float32 [4, 3072, 128], P(None, 'trace'), may hold values from -6 to 6
- green_interior: bfloat16 [4, 2, 4608, 3072], P('slab', None, 'trace'), may hold values from -0.078125 to 0.078125
- green_next: bfloat16 [4, 2, 3072, 3072], P('slab', None, 'trace'), may hold values from -0.0625 to 0.0625
- sources: float32 [4, 4, 3072, 128], P('slab', None, 'trace'), may hold values from -3 to 3
Outputs:
- interior: float32 [4, 4, 4608, 128], P('slab', None, 'trace')
- traces: float32 [4, 4, 3072, 128], P('slab', None, 'trace')
The draws below stay inside these ranges and needn't reach their ends.
All inputs are finite; a program needn't handle non-finite values.
Results may differ from the reference program's by a relative error of at most 0.014.
Values may be sent and summed in bfloat16 or wider, within the bound.
A program may use at most 64 MiB of HBM per device.

```python
import jax
import jax.numpy as jnp

TR = 3072
INTER = 4608
SRC = 64
FRONTS = 4
SLABS = 4
N_SLAB = 4


def shard_levels(stream_key, extent, cuts, smallest, largest):
    def one(axis_at, blocks):
        heights = jax.random.uniform(jax.random.fold_in(jax.random.fold_in(stream_key, 6), axis_at), (blocks,), jnp.float32, smallest / len(cuts), largest / len(cuts))
        return jnp.repeat(jnp.exp(heights), extent[axis_at] // blocks).reshape((-1,) + (1,) * (len(extent) - axis_at - 1))

    level = one(*cuts[0])
    for cut in cuts[1:]:
        level = level * one(*cut)
    return level


def noise(key, dims, scale, bound, shards=(), kind=jnp.bfloat16):
    factor_of = shard_levels(key, dims, shards, -0.22, 0.18) if shards else 1.0
    result = jax.random.normal(key, dims, jnp.float32) * scale * factor_of
    return jnp.minimum(jnp.maximum(result, -bound), bound).astype(kind)


def setup_inputs(seed: int = 0) -> dict:
    key_of = jax.random.split(jax.random.key(seed), 5)
    return {
        "incident": noise(key_of[0], (FRONTS, TR, 2 * SRC), 1.0, 6.0, ((1, 8),), jnp.float32),
        "green_interior": noise(key_of[1], (SLABS, 2, INTER, TR), (2 * TR) ** -0.5, 0.078125, ((0, 4), (2, 8))),
        "green_next": noise(key_of[2], (SLABS, 2, TR, TR), (5 * TR // 2) ** -0.5, 0.0625, ((0, 4), (2, 8))),
        "sources": noise(key_of[3], (SLABS, FRONTS, TR, 2 * SRC), 0.5, 3.0, ((0, 4), (2, 8)), jnp.float32),
    }


def complex_apply(halves, vectors, batches):
    row_count = halves.shape[1]
    inner_width = halves.shape[2]
    half_cols = vectors.shape[1] // (2 * batches)
    product = jnp.dot(halves.reshape(2 * row_count, inner_width), vectors, preferred_element_type=jnp.float32)
    product = product.reshape(2, row_count, batches, 2, half_cols)
    real_part = product[0, :, :, 0] - product[1, :, :, 1]
    imag_part = product[0, :, :, 1] + product[1, :, :, 0]
    return jnp.stack([real_part, imag_part], axis=2)


def to_fronts(product):
    row_count, batches, two_parts, half_cols = product.shape
    return jnp.transpose(product, (1, 0, 2, 3)).reshape(batches, row_count, two_parts * half_cols)


def reference(incident, green_interior, green_next, sources):
    current = jnp.transpose(incident, (1, 0, 2)).reshape(TR, FRONTS * 2 * SRC).astype(jnp.bfloat16)
    interiors = []
    outgoing = []
    for slab_index in range(N_SLAB):
        interiors.append(to_fronts(complex_apply(green_interior[slab_index], current, FRONTS)))
        leaving = to_fronts(complex_apply(green_next[slab_index], current, FRONTS)) + sources[slab_index]
        outgoing.append(leaving)
        current = jnp.transpose(leaving, (1, 0, 2)).reshape(TR, FRONTS * 2 * SRC).astype(jnp.bfloat16)
    return jnp.stack(interiors), jnp.stack(outgoing)
```

```python
import functools

import jax
import jax.numpy as jnp
from jax import lax
from jax.experimental import pallas as pl
from jax.experimental.pallas import tpu as pltpu
from jax.sharding import PartitionSpec as P

MESH = pl.DeviceIdType.MESH
INNER = 2
HALVES = 2
EARLY = 2
VMEM_LIMIT = 61 * 1024 * 1024


def chunk_count(blocks, rows):
    count = 4
    while count > 1 and (blocks % (count * INNER) or (blocks // count * rows) % 128):
        count //= 2
    return count


def flip(value, mask):
    result = value
    bit = 1
    while bit <= mask:
        if mask & bit:
            result = result + bit - 2 * bit * lax.rem(result // bit, 2)
        bit *= 2
    return result


def visit_order(count):
    return [0] + list(range(count - 1, 0, -1))


def group_of(fronts):
    return 2 if fronts % 2 == 0 else 1


def lanes(shape):
    return lax.broadcasted_iota(jnp.int32, shape, len(shape) - 1)


def turn(value, lead):
    columns = value.shape[-1]
    return pltpu.roll(value, (columns - lead) % columns, len(value.shape) - 1)


def split(value):
    quarter = value.shape[1] // 4
    lower = lanes(value.shape) < quarter
    near, far = turn(value, quarter), turn(value, 2 * quarter)
    return jnp.where(lower, value, near), jnp.where(lower, near, far)


def merge(first, second):
    quarter = first.shape[1] // 4
    lane = lanes(first.shape)
    low = jnp.where(lane < quarter, first, turn(second, -quarter))
    high = jnp.where(lane < 3 * quarter, turn(first, -quarter), turn(second, -2 * quarter))
    return jnp.where(lane < 2 * quarter, low, high)


def pack(value):
    rows, columns = value.shape
    lower, upper = value[: rows // 2], value[rows // 2 :]
    half = columns // 2
    return jnp.where(lanes(lower.shape) < half, lower, turn(upper, half)).astype(jnp.bfloat16)


def swap(packed):
    return pltpu.roll(packed, packed.shape[-1] // 2, len(packed.shape) - 1)


def rotate(first, second):
    quarter = first.shape[1] // 4
    real = lax.rem(lanes(first.shape) // quarter, 2) == 0
    return first + jnp.where(real, -turn(second, quarter), turn(second, -quarter))


def ordered(value):
    quarter = value.shape[1] // 4
    place = lanes(value.shape) // quarter
    return jnp.where(
        place == 1, turn(value, quarter), jnp.where(place == 2, turn(value, -quarter), value)
    )


def kernel(
    slabs,
    blocks,
    incident,
    green_interior,
    green_next,
    sources,
    interior,
    traces,
    entering,
    leaving,
    first_out,
    next_op,
    inner_op,
    incoming,
    own_sources,
    half_sources,
    half_out,
    next_sum,
    inner_sum,
    trace_out,
    inner_out,
    recv_sem,
    first_sem,
    direct_sem,
    relay_sem,
    load_sem,
    store_sem,
):
    parts, _, half_rows, columns = entering.shape
    fronts, rows = incoming.shape[:2]
    group = group_of(fronts)
    inner_rows = inner_op.shape[1]
    depth = next_op.shape[2]
    outer = blocks // INNER
    chunks = chunk_count(blocks, rows)
    per_chunk = blocks // chunks
    width = depth // chunks
    early = min(EARLY, parts)
    slab = lax.axis_index("slab")
    me = lax.axis_index("trace")
    lane_pos = lax.rem(me, INNER)
    my_outer = me // INNER
    partner = me + 1 - 2 * lane_pos
    first_slab = slab == 0
    second_slab = slab == 1
    last_slab = slab == slabs - 1
    my_chunk = me // per_chunk

    def load_incident(front):
        return pltpu.make_async_copy(
            incident.at[front], incoming.at[front], load_sem.at[3 + front]
        )

    load_next = pltpu.make_async_copy(green_next.at[0], next_op, load_sem.at[0])
    load_sources = pltpu.make_async_copy(sources.at[0], own_sources, load_sem.at[1])
    load_inner = pltpu.make_async_copy(green_interior.at[0], inner_op, load_sem.at[2])

    for front in range(fronts):
        load_incident(front).start()
    load_sources.start()
    load_next.start()
    load_inner.start()

    barrier = pltpu.get_barrier_semaphore()

    def greet(target_slab, target):
        pl.semaphore_signal(
            barrier, inc=1, device_id={"slab": target_slab, "trace": target}, device_id_type=MESH
        )

    def row_peer(step):
        return flip(my_outer, step) * INNER + lane_pos

    greet(slab, partner)

    @pl.when(first_slab)
    def _():
        for step in range(1, outer):
            greet(1, row_peer(step))
            greet(slabs - 1, row_peer(step))

    @pl.when(jnp.logical_not(first_slab))
    def _():
        for step in range(outer):
            greet(slab - 1, row_peer(step))

    peers = 1 + jnp.where(last_slab, outer - 1, outer) + jnp.where(second_slab, outer - 1, 0)
    pl.semaphore_wait(barrier, peers)

    def first_copy(part, step):
        return pltpu.make_async_remote_copy(
            src_ref=first_out.at[part],
            dst_ref=entering.at[part, me],
            send_sem=first_sem.at[part, step],
            recv_sem=recv_sem.at[part, me],
            device_id={"slab": 0, "trace": row_peer(step)},
            device_id_type=MESH,
        )

    def next_copy(part, step):
        return pltpu.make_async_remote_copy(
            src_ref=leaving.at[part],
            dst_ref=entering.at[part, me],
            send_sem=direct_sem.at[part, step],
            recv_sem=recv_sem.at[part, me],
            device_id={"slab": slab + 1, "trace": row_peer(step)},
            device_id_type=MESH,
        )

    def relay_copy(part, block):
        return pltpu.make_async_remote_copy(
            src_ref=entering.at[part, block],
            dst_ref=entering.at[part, block],
            send_sem=relay_sem.at[part, block // INNER],
            recv_sem=recv_sem.at[part, block],
            device_id={"slab": slab, "trace": partner},
            device_id_type=MESH,
        )

    def store_trace(front):
        return pltpu.make_async_copy(
            trace_out.at[front], traces.at[0, front], store_sem.at[0, front]
        )

    def store_inner(front):
        return pltpu.make_async_copy(
            inner_out.at[front], interior.at[0, front], store_sem.at[1, front]
        )

    for front in range(fronts):
        load_incident(front).wait()

    @pl.when(first_slab)
    def _():
        for front in range(fronts):
            for index, value in enumerate(split(incoming[front])):
                entering[HALVES * front + index, me] = pack(value)

    def send_first(start, stop):
        for part in range(start, stop):
            first_out[part] = pack(split(incoming[part // HALVES])[part % HALVES])
            for step in visit_order(outer)[1:]:
                first_copy(part, step).start()

    @pl.when(second_slab)
    def _():
        send_first(0, early)

    @pl.when(last_slab)
    def _():
        send_first(early, parts)

    def chunk_at(order):
        return flip(my_chunk, visit_order(chunks)[order])

    def relay_chunk(part, order):
        for index in range(per_chunk // INNER):
            block = chunk_at(order) * per_chunk + index * INNER + lane_pos

            @pl.when(jnp.logical_not(first_slab & (block == me)))
            def _():
                relay_copy(part, block).wait_recv()

            relay_copy(part, block).start()

    def await_relayed(part, order):
        for index in range(per_chunk // INNER):
            block = chunk_at(order) * per_chunk + index * INNER + 1 - lane_pos
            relay_copy(part, block).wait_recv()

    def packed_rows(part, chunk):
        return entering[part, pl.ds(chunk * per_chunk, per_chunk)]

    def stacked(lower, upper):
        return jnp.concatenate([lower, upper], axis=1).reshape(width, columns)

    def matrix_of(op, chunk):
        start = pl.multiple_of(chunk * width, width)
        return op[:, :, pl.ds(start, width)].reshape(2 * op.shape[1], width)

    def next_chunk(part, order):
        chunk = chunk_at(order)
        value = packed_rows(part, chunk)
        product = jnp.dot(
            matrix_of(next_op, chunk),
            stacked(value, swap(value)),
            preferred_element_type=jnp.float32,
        )
        if order == 0:
            next_sum[...] = product
        else:
            next_sum[...] += product

    def inner_chunk(front, chunk, fresh):
        both = []
        for index in range(group):
            low = packed_rows(HALVES * (front + index), chunk)
            high = packed_rows(HALVES * (front + index) + 1, chunk)
            lower = lanes(low.shape) < columns // 2
            both.append(
                stacked(jnp.where(lower, low, swap(high)), jnp.where(lower, swap(low), high))
            )
        product = jnp.dot(
            matrix_of(inner_op, chunk),
            jnp.concatenate(both, axis=1),
            preferred_element_type=jnp.float32,
        )
        if fresh:
            inner_sum[...] = product
        else:
            inner_sum[...] += product

    def inner_finish(front):
        for index in range(group):
            place = pl.ds(index * columns, columns)
            result = rotate(inner_sum[0:inner_rows, place], inner_sum[inner_rows:, place])
            inner_out[front + index] = ordered(result)
            store_inner(front + index).start()

    def inner_group(front):
        inner_chunk(front, 0, True)

        def more(chunk, carry):
            inner_chunk(front, chunk, False)
            return carry

        lax.fori_loop(1, chunks, more, 0)
        inner_finish(front)

    for order in range(chunks):
        relay_chunk(0, order)

    load_sources.wait()
    for front in range(fronts):
        for index, value in enumerate(split(own_sources[front])):
            half_sources[HALVES * front + index] = value
    load_next.wait()
    load_inner.wait()

    def one_part(part, carry):
        closing = part == parts - 1
        side = lax.rem(part, HALVES)
        front = part // HALVES
        for order in range(chunks):
            await_relayed(part, order)
            next_chunk(part, order)

            @pl.when(closing & last_slab)
            def _():
                inner_chunk(fronts - group, chunk_at(order), order == 0)

            @pl.when(jnp.logical_not(closing))
            def _():
                relay_chunk(part + 1, order)

        result = rotate(next_sum[0:rows], next_sum[rows:]) + half_sources[part]
        leaving[part] = pack(result)

        @pl.when(jnp.logical_not(last_slab))
        def _():
            for step in visit_order(outer):
                next_copy(part, step).start()

        half_out[side] = result

        @pl.when(side == HALVES - 1)
        def _():
            trace_out[front] = merge(half_out[0], half_out[1])
            store_trace(front).start()

        full = lax.rem(part, group * HALVES) == group * HALVES - 1

        @pl.when(full & last_slab & jnp.logical_not(closing))
        def _():
            inner_group(front + 1 - group)

        return carry

    lax.fori_loop(0, parts, one_part, 0)

    @pl.when(last_slab)
    def _():
        inner_finish(fronts - group)

    @pl.when(jnp.logical_not(last_slab))
    def _():
        def rest(index, carry):
            inner_group(index * group)
            return carry

        lax.fori_loop(0, fronts // group, rest, 0)

    def drain_first(start, stop):
        for part in range(start, stop):
            for step in range(1, outer):
                first_copy(part, step).wait_send()

    @pl.when(second_slab)
    def _():
        drain_first(0, early)

    @pl.when(last_slab)
    def _():
        drain_first(early, parts)

    def drain(part, carry):
        @pl.when(jnp.logical_not(last_slab))
        def _():
            for step in range(outer):
                next_copy(part, step).wait_send()

        for index in range(outer):
            relay_copy(part, index * INNER + lane_pos).wait_send()
        return carry

    lax.fori_loop(0, parts, drain, 0)
    for front in range(fronts):
        store_trace(front).wait()
        store_inner(front).wait()


def local(slabs, blocks, incident, green_interior, green_next, sources):
    fronts, rows, columns = incident.shape
    parts, half_rows = HALVES * fronts, rows // HALVES
    inner_rows = green_interior.shape[2]
    depth = green_next.shape[3]
    outer = blocks // INNER
    in_hbm = pl.BlockSpec(memory_space=pltpu.HBM)
    anywhere = pl.BlockSpec(memory_space=pl.ANY)
    return pl.pallas_call(
        functools.partial(kernel, slabs, blocks),
        out_shape=(
            jax.ShapeDtypeStruct((1, fronts, inner_rows, columns), jnp.float32),
            jax.ShapeDtypeStruct((1, fronts, rows, columns), jnp.float32),
        ),
        in_specs=[in_hbm] * 4,
        out_specs=(anywhere, anywhere),
        scratch_shapes=[
            pltpu.VMEM((parts, blocks, half_rows, columns), jnp.bfloat16),
            pltpu.VMEM((parts, half_rows, columns), jnp.bfloat16),
            pltpu.VMEM((parts, half_rows, columns), jnp.bfloat16),
            pltpu.VMEM((2, rows, depth), jnp.bfloat16),
            pltpu.VMEM((2, inner_rows, depth), jnp.bfloat16),
            pltpu.VMEM((fronts, rows, columns), jnp.float32),
            pltpu.VMEM((fronts, rows, columns), jnp.float32),
            pltpu.VMEM((parts, rows, columns), jnp.float32),
            pltpu.VMEM((HALVES, rows, columns), jnp.float32),
            pltpu.VMEM((2 * rows, columns), jnp.float32),
            pltpu.VMEM((2 * inner_rows, group_of(fronts) * columns), jnp.float32),
            pltpu.VMEM((fronts, rows, columns), jnp.float32),
            pltpu.VMEM((fronts, inner_rows, columns), jnp.float32),
            pltpu.SemaphoreType.DMA((parts, blocks)),
            pltpu.SemaphoreType.DMA((parts, outer)),
            pltpu.SemaphoreType.DMA((parts, outer)),
            pltpu.SemaphoreType.DMA((parts, outer)),
            pltpu.SemaphoreType.DMA((3 + fronts,)),
            pltpu.SemaphoreType.DMA((2, fronts)),
        ],
        compiler_params=pltpu.CompilerParams(
            collective_id=0, has_side_effects=True, vmem_limit_bytes=VMEM_LIMIT
        ),
    )(incident, green_interior, green_next, sources)


def solution(mesh):
    return jax.shard_map(
        functools.partial(local, mesh.shape["slab"], mesh.shape["trace"]),
        mesh=mesh,
        in_specs=(
            P(None, "trace", None),
            P("slab", None, "trace", None),
            P("slab", None, "trace", None),
            P("slab", None, "trace", None),
        ),
        out_specs=(P("slab", None, "trace", None), P("slab", None, "trace", None)),
        check_vma=False,
    )
```

```python
import functools

import jax
import jax.numpy as jnp
from jax import lax
from jax.experimental import pallas as pl
from jax.experimental.pallas import tpu as pltpu
from jax.sharding import PartitionSpec as P

MESH = pl.DeviceIdType.MESH
INNER = 2
HALVES = 2
EARLY = 2
VMEM_LIMIT = 48 * 1024 * 1024


def chunk_count(blocks, rows):
    count = 4
    while count > 1 and (blocks % (count * INNER) or (blocks // count * rows) % 128):
        count //= 2
    return count


def flip(value, mask):
    result = value
    bit = 1
    while bit <= mask:
        if mask & bit:
            result = result + bit - 2 * bit * lax.rem(result // bit, 2)
        bit *= 2
    return result


def visit_order(count):
    return [0] + list(range(count - 1, 0, -1))


def group_of(fronts):
    return 2 if fronts % 2 == 0 else 1


def lanes(shape):
    return lax.broadcasted_iota(jnp.int32, shape, len(shape) - 1)


def turn(value, lead):
    columns = value.shape[-1]
    return pltpu.roll(value, (columns - lead) % columns, len(value.shape) - 1)


def split(value):
    quarter = value.shape[1] // 4
    lower = lanes(value.shape) < quarter
    near, far = turn(value, quarter), turn(value, 2 * quarter)
    return jnp.where(lower, value, near), jnp.where(lower, near, far)


def merge(first, second):
    quarter = first.shape[1] // 4
    lane = lanes(first.shape)
    low = jnp.where(lane < quarter, first, turn(second, -quarter))
    high = jnp.where(lane < 3 * quarter, turn(first, -quarter), turn(second, -2 * quarter))
    return jnp.where(lane < 2 * quarter, low, high)


def pack(value):
    rows, columns = value.shape
    lower, upper = value[: rows // 2], value[rows // 2 :]
    half = columns // 2
    return jnp.where(lanes(lower.shape) < half, lower, turn(upper, half)).astype(jnp.bfloat16)


def swap(packed):
    return pltpu.roll(packed, packed.shape[-1] // 2, len(packed.shape) - 1)


def rotate(first, second):
    quarter = first.shape[1] // 4
    real = lax.rem(lanes(first.shape) // quarter, 2) == 0
    return first + jnp.where(real, -turn(second, quarter), turn(second, -quarter))


def ordered(value):
    quarter = value.shape[1] // 4
    place = lanes(value.shape) // quarter
    return jnp.where(
        place == 1, turn(value, quarter), jnp.where(place == 2, turn(value, -quarter), value)
    )


def kernel(
    slabs,
    blocks,
    incident,
    green_interior,
    green_next,
    sources,
    interior,
    traces,
    entering,
    leaving,
    first_out,
    next_op,
    inner_op,
    incoming,
    own_sources,
    half_sources,
    half_out,
    next_sum,
    inner_sum,
    trace_out,
    inner_out,
    recv_sem,
    first_sem,
    direct_sem,
    relay_sem,
    load_sem,
    store_sem,
):
    parts, _, half_rows, columns = entering.shape
    fronts, rows = incoming.shape[:2]
    group = group_of(fronts)
    inner_rows = inner_op.shape[1]
    depth = next_op.shape[2]
    outer = blocks // INNER
    chunks = chunk_count(blocks, rows)
    per_chunk = blocks // chunks
    width = depth // chunks
    early = min(EARLY, parts)
    slab = lax.axis_index("slab")
    me = lax.axis_index("trace")
    lane_pos = lax.rem(me, INNER)
    my_outer = me // INNER
    partner = me + 1 - 2 * lane_pos
    first_slab = slab == 0
    second_slab = slab == 1
    last_slab = slab == slabs - 1
    my_chunk = me // per_chunk

    def load_incident(front):
        return pltpu.make_async_copy(
            incident.at[front], incoming.at[front], load_sem.at[3 + front]
        )

    load_next = pltpu.make_async_copy(green_next.at[0], next_op, load_sem.at[0])
    load_sources = pltpu.make_async_copy(sources.at[0], own_sources, load_sem.at[1])
    load_inner = pltpu.make_async_copy(green_interior.at[0], inner_op, load_sem.at[2])

    for front in range(fronts):
        load_incident(front).start()
    load_sources.start()
    load_next.start()
    load_inner.start()

    barrier = pltpu.get_barrier_semaphore()

    def greet(target_slab, target):
        pl.semaphore_signal(
            barrier, inc=1, device_id={"slab": target_slab, "trace": target}, device_id_type=MESH
        )

    def row_peer(step):
        return flip(my_outer, step) * INNER + lane_pos

    greet(slab, partner)

    @pl.when(first_slab)
    def _():
        for step in range(1, outer):
            greet(1, row_peer(step))
            greet(slabs - 1, row_peer(step))

    @pl.when(jnp.logical_not(first_slab))
    def _():
        for step in range(outer):
            greet(slab - 1, row_peer(step))

    peers = 1 + jnp.where(last_slab, outer - 1, outer) + jnp.where(second_slab, outer - 1, 0)
    pl.semaphore_wait(barrier, peers)

    def first_copy(part, step):
        return pltpu.make_async_remote_copy(
            src_ref=first_out.at[part],
            dst_ref=entering.at[part, me],
            send_sem=first_sem.at[part, step],
            recv_sem=recv_sem.at[part, me],
            device_id={"slab": 0, "trace": row_peer(step)},
            device_id_type=MESH,
        )

    def next_copy(part, step):
        return pltpu.make_async_remote_copy(
            src_ref=leaving.at[part],
            dst_ref=entering.at[part, me],
            send_sem=direct_sem.at[part, step],
            recv_sem=recv_sem.at[part, me],
            device_id={"slab": slab + 1, "trace": row_peer(step)},
            device_id_type=MESH,
        )

    def relay_copy(part, block):
        return pltpu.make_async_remote_copy(
            src_ref=entering.at[part, block],
            dst_ref=entering.at[part, block],
            send_sem=relay_sem.at[part, block // INNER],
            recv_sem=recv_sem.at[part, block],
            device_id={"slab": slab, "trace": partner},
            device_id_type=MESH,
        )

    def store_trace(front):
        return pltpu.make_async_copy(
            trace_out.at[front], traces.at[0, front], store_sem.at[0, front]
        )

    def store_inner(front):
        return pltpu.make_async_copy(
            inner_out.at[front], interior.at[0, front], store_sem.at[1, front]
        )

    for front in range(fronts):
        load_incident(front).wait()

    @pl.when(first_slab)
    def _():
        for front in range(fronts):
            for index, value in enumerate(split(incoming[front])):
                entering[HALVES * front + index, me] = pack(value)

    def send_first(start, stop):
        for part in range(start, stop):
            first_out[part] = pack(split(incoming[part // HALVES])[part % HALVES])
            for step in visit_order(outer)[1:]:
                first_copy(part, step).start()

    @pl.when(second_slab)
    def _():
        send_first(0, early)

    @pl.when(last_slab)
    def _():
        send_first(early, parts)

    def chunk_at(order):
        return flip(my_chunk, visit_order(chunks)[order])

    def relay_chunk(part, order):
        for index in range(per_chunk // INNER):
            block = chunk_at(order) * per_chunk + index * INNER + lane_pos

            @pl.when(jnp.logical_not(first_slab & (block == me)))
            def _():
                relay_copy(part, block).wait_recv()

            relay_copy(part, block).start()

    def await_relayed(part, order):
        for index in range(per_chunk // INNER):
            block = chunk_at(order) * per_chunk + index * INNER + 1 - lane_pos
            relay_copy(part, block).wait_recv()

    def packed_rows(part, chunk):
        return entering[part, pl.ds(chunk * per_chunk, per_chunk)]

    def stacked(lower, upper):
        return jnp.concatenate([lower, upper], axis=1).reshape(width, columns)

    def matrix_of(op, chunk):
        start = pl.multiple_of(chunk * width, width)
        return op[:, :, pl.ds(start, width)].reshape(2 * op.shape[1], width)

    def next_chunk(part, order):
        chunk = chunk_at(order)
        value = packed_rows(part, chunk)
        product = jnp.dot(
            matrix_of(next_op, chunk),
            stacked(value, swap(value)),
            preferred_element_type=jnp.float32,
        )
        if order == 0:
            next_sum[...] = product
        else:
            next_sum[...] += product

    def inner_chunk(front, chunk, fresh):
        both = []
        for index in range(group):
            low = packed_rows(HALVES * (front + index), chunk)
            high = packed_rows(HALVES * (front + index) + 1, chunk)
            lower = lanes(low.shape) < columns // 2
            both.append(
                stacked(jnp.where(lower, low, swap(high)), jnp.where(lower, swap(low), high))
            )
        product = jnp.dot(
            matrix_of(inner_op, chunk),
            jnp.concatenate(both, axis=1),
            preferred_element_type=jnp.float32,
        )
        if fresh:
            inner_sum[...] = product
        else:
            inner_sum[...] += product

    def inner_finish(front):
        for index in range(group):
            place = pl.ds(index * columns, columns)
            result = rotate(inner_sum[0:inner_rows, place], inner_sum[inner_rows:, place])
            inner_out[front + index] = ordered(result)
            store_inner(front + index).start()

    def inner_group(front):
        inner_chunk(front, 0, True)

        def more(chunk, carry):
            inner_chunk(front, chunk, False)
            return carry

        lax.fori_loop(1, chunks, more, 0)
        inner_finish(front)

    for order in range(chunks):
        relay_chunk(0, order)

    load_sources.wait()
    for front in range(fronts):
        for index, value in enumerate(split(own_sources[front])):
            half_sources[HALVES * front + index] = value
    load_next.wait()
    load_inner.wait()

    def one_part(part, carry):
        closing = part == parts - 1
        side = lax.rem(part, HALVES)
        front = part // HALVES
        for order in range(chunks):
            await_relayed(part, order)
            next_chunk(part, order)

            @pl.when(closing & last_slab)
            def _():
                inner_chunk(fronts - group, chunk_at(order), order == 0)

            @pl.when(jnp.logical_not(closing))
            def _():
                relay_chunk(part + 1, order)

        result = rotate(next_sum[0:rows], next_sum[rows:]) + half_sources[part]
        leaving[part] = pack(result)

        @pl.when(jnp.logical_not(last_slab))
        def _():
            for step in visit_order(outer):
                next_copy(part, step).start()

        half_out[side] = result

        @pl.when(side == HALVES - 1)
        def _():
            trace_out[front] = merge(half_out[0], half_out[1])
            store_trace(front).start()

        full = lax.rem(part, group * HALVES) == group * HALVES - 1

        @pl.when(full & last_slab & jnp.logical_not(closing))
        def _():
            inner_group(front + 1 - group)

        return carry

    lax.fori_loop(0, parts, one_part, 0)

    @pl.when(last_slab)
    def _():
        inner_finish(fronts - group)

    @pl.when(jnp.logical_not(last_slab))
    def _():
        def rest(index, carry):
            inner_group(index * group)
            return carry

        lax.fori_loop(0, fronts // group, rest, 0)

    def drain_first(start, stop):
        for part in range(start, stop):
            for step in range(1, outer):
                first_copy(part, step).wait_send()

    @pl.when(second_slab)
    def _():
        drain_first(0, early)

    @pl.when(last_slab)
    def _():
        drain_first(early, parts)

    def drain(part, carry):
        @pl.when(jnp.logical_not(last_slab))
        def _():
            for step in range(outer):
                next_copy(part, step).wait_send()

        for index in range(outer):
            relay_copy(part, index * INNER + lane_pos).wait_send()
        return carry

    lax.fori_loop(0, parts, drain, 0)
    for front in range(fronts):
        store_trace(front).wait()
        store_inner(front).wait()


def local(slabs, blocks, incident, green_interior, green_next, sources):
    fronts, rows, columns = incident.shape
    parts, half_rows = HALVES * fronts, rows // HALVES
    inner_rows = green_interior.shape[2]
    depth = green_next.shape[3]
    outer = blocks // INNER
    in_hbm = pl.BlockSpec(memory_space=pltpu.HBM)
    incident = pltpu.with_memory_space_constraint(incident, pltpu.HBM)
    sources = pltpu.with_memory_space_constraint(sources, pltpu.HBM)
    anywhere = pl.BlockSpec(memory_space=pl.ANY)
    return pl.pallas_call(
        functools.partial(kernel, slabs, blocks),
        out_shape=(
            jax.ShapeDtypeStruct((1, fronts, inner_rows, columns), jnp.float32),
            jax.ShapeDtypeStruct((1, fronts, rows, columns), jnp.float32),
        ),
        in_specs=[in_hbm] * 4,
        out_specs=(anywhere, anywhere),
        scratch_shapes=[
            pltpu.VMEM((parts, blocks, half_rows, columns), jnp.bfloat16),
            pltpu.VMEM((parts, half_rows, columns), jnp.bfloat16),
            pltpu.VMEM((parts, half_rows, columns), jnp.bfloat16),
            pltpu.VMEM((2, rows, depth), jnp.bfloat16),
            pltpu.VMEM((2, inner_rows, depth), jnp.bfloat16),
            pltpu.VMEM((fronts, rows, columns), jnp.float32),
            pltpu.VMEM((fronts, rows, columns), jnp.float32),
            pltpu.VMEM((parts, rows, columns), jnp.float32),
            pltpu.VMEM((HALVES, rows, columns), jnp.float32),
            pltpu.VMEM((2 * rows, columns), jnp.float32),
            pltpu.VMEM((2 * inner_rows, group_of(fronts) * columns), jnp.float32),
            pltpu.VMEM((fronts, rows, columns), jnp.float32),
            pltpu.VMEM((fronts, inner_rows, columns), jnp.float32),
            pltpu.SemaphoreType.DMA((parts, blocks)),
            pltpu.SemaphoreType.DMA((parts, outer)),
            pltpu.SemaphoreType.DMA((parts, outer)),
            pltpu.SemaphoreType.DMA((parts, outer)),
            pltpu.SemaphoreType.DMA((3 + fronts,)),
            pltpu.SemaphoreType.DMA((2, fronts)),
        ],
        compiler_params=pltpu.CompilerParams(
            collective_id=0, has_side_effects=True, vmem_limit_bytes=VMEM_LIMIT
        ),
    )(incident, green_interior, green_next, sources)


def solution(mesh):
    return jax.shard_map(
        functools.partial(local, mesh.shape["slab"], mesh.shape["trace"]),
        mesh=mesh,
        in_specs=(
            P(None, "trace", None),
            P("slab", None, "trace", None),
            P("slab", None, "trace", None),
            P("slab", None, "trace", None),
        ),
        out_specs=(P("slab", None, "trace", None), P("slab", None, "trace", None)),
        check_vma=False,
    )
```

```python
import functools

import jax
import jax.numpy as jnp
from jax import lax
from jax.experimental import pallas as pl
from jax.experimental.pallas import tpu as pltpu
from jax.sharding import PartitionSpec as P

MESH = pl.DeviceIdType.MESH
INNER = 2
HALVES = 2
EARLY = 2
OWN = 4
VMEM_LIMIT = 48 * 1024 * 1024


def chunk_count(blocks, rows):
    count = 4
    while count > 1 and (blocks % (count * INNER) or (blocks // count * rows) % 128):
        count //= 2
    return count


def flip(value, mask):
    result = value
    bit = 1
    while bit <= mask:
        if mask & bit:
            result = result + bit - 2 * bit * lax.rem(result // bit, 2)
        bit *= 2
    return result


def visit_order(count):
    return [0] + list(range(count - 1, 0, -1))


def compute_order(count):
    return [0, 1][:count] + list(range(count - 1, 1, -1))


def group_of(fronts):
    return 2 if fronts % 2 == 0 else 1


def lanes(shape):
    return lax.broadcasted_iota(jnp.int32, shape, len(shape) - 1)


def turn(value, lead):
    columns = value.shape[-1]
    return pltpu.roll(value, (columns - lead) % columns, len(value.shape) - 1)


def split(value):
    quarter = value.shape[1] // 4
    lower = lanes(value.shape) < quarter
    near, far = turn(value, quarter), turn(value, 2 * quarter)
    return jnp.where(lower, value, near), jnp.where(lower, near, far)


def merge(first, second):
    quarter = first.shape[1] // 4
    lane = lanes(first.shape)
    low = jnp.where(lane < quarter, first, turn(second, -quarter))
    high = jnp.where(lane < 3 * quarter, turn(first, -quarter), turn(second, -2 * quarter))
    return jnp.where(lane < 2 * quarter, low, high)


def pack(value):
    rows, columns = value.shape
    lower, upper = value[: rows // 2], value[rows // 2 :]
    half = columns // 2
    return jnp.where(lanes(lower.shape) < half, lower, turn(upper, half)).astype(jnp.bfloat16)


def swap(packed):
    return pltpu.roll(packed, packed.shape[-1] // 2, len(packed.shape) - 1)


def rotate(first, second):
    quarter = first.shape[1] // 4
    real = lax.rem(lanes(first.shape) // quarter, 2) == 0
    return first + jnp.where(real, -turn(second, quarter), turn(second, -quarter))


def ordered(value):
    quarter = value.shape[1] // 4
    place = lanes(value.shape) // quarter
    return jnp.where(
        place == 1, turn(value, quarter), jnp.where(place == 2, turn(value, -quarter), value)
    )


def kernel(
    slabs,
    blocks,
    incident,
    green_interior,
    green_next,
    sources,
    interior,
    traces,
    entering,
    leaving,
    first_out,
    next_op,
    inner_op,
    incoming,
    own_sources,
    half_sources,
    half_out,
    next_sum,
    inner_sum,
    trace_out,
    inner_out,
    recv_sem,
    first_sem,
    direct_sem,
    relay_sem,
    load_sem,
    store_sem,
):
    parts, _, half_rows, columns = entering.shape
    fronts, rows = incoming.shape[:2]
    group = group_of(fronts)
    inner_rows = inner_op.shape[1]
    depth = next_op.shape[2]
    outer = blocks // INNER
    chunks = chunk_count(blocks, rows)
    per_chunk = blocks // chunks
    width = depth // chunks
    early = min(EARLY, parts)
    slab = lax.axis_index("slab")
    me = lax.axis_index("trace")
    lane_pos = lax.rem(me, INNER)
    my_outer = me // INNER
    partner = me + 1 - 2 * lane_pos
    first_slab = slab == 0
    second_slab = slab == 1
    last_slab = slab == slabs - 1
    my_chunk = me // per_chunk

    def load_incident(front):
        return pltpu.make_async_copy(
            incident.at[front], incoming.at[front], load_sem.at[3 + front]
        )

    load_next = pltpu.make_async_copy(green_next.at[0], next_op, load_sem.at[0])
    load_sources = pltpu.make_async_copy(sources.at[0], own_sources, load_sem.at[1])
    load_inner = pltpu.make_async_copy(green_interior.at[0], inner_op, load_sem.at[2])

    for front in range(fronts):
        load_incident(front).start()
    load_sources.start()
    load_next.start()
    load_inner.start()

    barrier = pltpu.get_barrier_semaphore()

    def greet(target_slab, target):
        pl.semaphore_signal(
            barrier, inc=1, device_id={"slab": target_slab, "trace": target}, device_id_type=MESH
        )

    def row_peer(step):
        return flip(my_outer, step) * INNER + lane_pos

    greet(slab, partner)
    greet(slab, row_peer(1))

    @pl.when(first_slab)
    def _():
        for step in range(1, outer):
            greet(1, row_peer(step))
            greet(slabs - 1, row_peer(step))

    @pl.when(jnp.logical_not(first_slab))
    def _():
        greet(slab - 1, partner)
        for step in range(outer):
            greet(slab - 1, row_peer(step))

    peers = 2 + jnp.where(last_slab, outer - 1, outer + 1) + jnp.where(second_slab, outer - 1, 0)
    pl.semaphore_wait(barrier, peers)

    def first_copy(part, step):
        return pltpu.make_async_remote_copy(
            src_ref=first_out.at[part],
            dst_ref=entering.at[part, me],
            send_sem=first_sem.at[part, step],
            recv_sem=recv_sem.at[part, me],
            device_id={"slab": 0, "trace": row_peer(step)},
            device_id_type=MESH,
        )

    def next_copy(part, step):
        return pltpu.make_async_remote_copy(
            src_ref=leaving.at[part],
            dst_ref=entering.at[part, me],
            send_sem=direct_sem.at[part, step],
            recv_sem=recv_sem.at[part, me],
            device_id={"slab": slab + 1, "trace": row_peer(step)},
            device_id_type=MESH,
        )

    def side_copy(part):
        return pltpu.make_async_remote_copy(
            src_ref=leaving.at[part],
            dst_ref=entering.at[part, me],
            send_sem=direct_sem.at[part, outer],
            recv_sem=recv_sem.at[part, me],
            device_id={"slab": slab + 1, "trace": partner},
            device_id_type=MESH,
        )

    def row_copy(part):
        return pltpu.make_async_remote_copy(
            src_ref=entering.at[part, partner],
            dst_ref=entering.at[part, partner],
            send_sem=relay_sem.at[part, flip(my_outer, 1)],
            recv_sem=recv_sem.at[part, partner],
            device_id={"slab": slab, "trace": row_peer(1)},
            device_id_type=MESH,
        )

    def relay_copy(part, block):
        return pltpu.make_async_remote_copy(
            src_ref=entering.at[part, block],
            dst_ref=entering.at[part, block],
            send_sem=relay_sem.at[part, block // INNER],
            recv_sem=recv_sem.at[part, block],
            device_id={"slab": slab, "trace": partner},
            device_id_type=MESH,
        )

    def store_trace(front):
        return pltpu.make_async_copy(
            trace_out.at[front], traces.at[0, front], store_sem.at[0, front]
        )

    def store_inner(front):
        return pltpu.make_async_copy(
            inner_out.at[front], interior.at[0, front], store_sem.at[1, front]
        )

    for front in range(fronts):
        load_incident(front).wait()

    @pl.when(first_slab)
    def _():
        for front in range(fronts):
            for index, value in enumerate(split(incoming[front])):
                entering[HALVES * front + index, me] = pack(value)

    def send_first(start, stop):
        for part in range(start, stop):
            first_out[part] = pack(split(incoming[part // HALVES])[part % HALVES])
            for step in visit_order(outer)[1:]:
                first_copy(part, step).start()

    @pl.when(second_slab)
    def _():
        send_first(0, early)

    @pl.when(last_slab)
    def _():
        send_first(early, parts)

    def steps_of(place):
        span = per_chunk // INNER
        return range(place * span, (place + 1) * span)

    def relay_chunk(part, order):
        for step in steps_of(visit_order(chunks)[order]):
            if step == 0:

                @pl.when(first_slab & (part + OWN < parts))
                def _():
                    relay_copy(part + OWN, me).start()

                relay_copy(part, partner).wait_recv()
                row_copy(part).start()
            elif step > 1:
                relay_copy(part, row_peer(step)).wait_recv()
                relay_copy(part, row_peer(step)).start()

    def await_chunk(part, place):
        for step in steps_of(place):
            mine = row_peer(step)
            other = mine + 1 - 2 * lane_pos
            if step == 0:

                @pl.when(jnp.logical_not(first_slab))
                def _():
                    relay_copy(part, mine).wait_recv()

            else:
                if step == 1:
                    relay_copy(part, mine).wait_recv()
                relay_copy(part, other).wait_recv()

    def packed_rows(part, chunk):
        return entering[part, pl.ds(chunk * per_chunk, per_chunk)]

    def stacked(lower, upper):
        return jnp.concatenate([lower, upper], axis=1).reshape(width, columns)

    def matrix_of(op, chunk):
        start = pl.multiple_of(chunk * width, width)
        return op[:, :, pl.ds(start, width)].reshape(2 * op.shape[1], width)

    def next_chunk(part, place):
        chunk = flip(my_chunk, place)
        value = packed_rows(part, chunk)
        product = jnp.dot(
            matrix_of(next_op, chunk),
            stacked(value, swap(value)),
            preferred_element_type=jnp.float32,
        )
        if place == 0:
            next_sum[...] = product
        else:
            next_sum[...] += product

    def inner_chunk(front, chunk, fresh):
        both = []
        for index in range(group):
            low = packed_rows(HALVES * (front + index), chunk)
            high = packed_rows(HALVES * (front + index) + 1, chunk)
            lower = lanes(low.shape) < columns // 2
            both.append(
                stacked(jnp.where(lower, low, swap(high)), jnp.where(lower, swap(low), high))
            )
        product = jnp.dot(
            matrix_of(inner_op, chunk),
            jnp.concatenate(both, axis=1),
            preferred_element_type=jnp.float32,
        )
        if fresh:
            inner_sum[...] = product
        else:
            inner_sum[...] += product

    def inner_finish(front):
        for index in range(group):
            place = pl.ds(index * columns, columns)
            result = rotate(inner_sum[0:inner_rows, place], inner_sum[inner_rows:, place])
            inner_out[front + index] = ordered(result)
            store_inner(front + index).start()

    def inner_group(front):
        inner_chunk(front, 0, True)

        def more(chunk, carry):
            inner_chunk(front, chunk, False)
            return carry

        lax.fori_loop(1, chunks, more, 0)
        inner_finish(front)

    def relay_ahead(part, order):
        for lead, mine in leads:
            step, later = divmod(order + lead, chunks)

            @pl.when(mine & (part + step < parts))
            def _():
                relay_chunk(part + step, later)

    @pl.when(first_slab)
    def _():
        for part in range(min(OWN, parts)):
            relay_copy(part, me).start()

    leads = [(6, first_slab), (4, jnp.logical_not(first_slab))]
    for lead, mine in leads:

        @pl.when(mine)
        def _():
            for count in range(lead):
                relay_chunk(count // chunks, count % chunks)

    load_sources.wait()
    for front in range(fronts):
        for index, value in enumerate(split(own_sources[front])):
            half_sources[HALVES * front + index] = value
    load_next.wait()
    load_inner.wait()

    def one_part(part, carry):
        closing = part == parts - 1
        side = lax.rem(part, HALVES)
        front = part // HALVES
        for order, place in enumerate(compute_order(chunks)):
            await_chunk(part, place)
            next_chunk(part, place)

            @pl.when(closing & last_slab)
            def _():
                inner_chunk(fronts - group, flip(my_chunk, place), order == 0)

            relay_ahead(part, order)

        result = rotate(next_sum[0:rows], next_sum[rows:]) + half_sources[part]
        leaving[part] = pack(result)

        @pl.when(jnp.logical_not(last_slab))
        def _():
            next_copy(part, 0).start()
            side_copy(part).start()
            for step in visit_order(outer)[1:]:
                next_copy(part, step).start()

        half_out[side] = result

        @pl.when(side == HALVES - 1)
        def _():
            trace_out[front] = merge(half_out[0], half_out[1])
            store_trace(front).start()

        full = lax.rem(part, group * HALVES) == group * HALVES - 1

        @pl.when(full & last_slab & jnp.logical_not(closing))
        def _():
            inner_group(front + 1 - group)

        return carry

    lax.fori_loop(0, parts, one_part, 0)

    @pl.when(last_slab)
    def _():
        inner_finish(fronts - group)

    @pl.when(jnp.logical_not(last_slab))
    def _():
        def rest(index, carry):
            inner_group(index * group)
            return carry

        lax.fori_loop(0, fronts // group, rest, 0)

    def drain_first(start, stop):
        for part in range(start, stop):
            for step in range(1, outer):
                first_copy(part, step).wait_send()

    @pl.when(second_slab)
    def _():
        drain_first(0, early)

    @pl.when(last_slab)
    def _():
        drain_first(early, parts)

    def drain(part, carry):
        @pl.when(jnp.logical_not(last_slab))
        def _():
            side_copy(part).wait_send()
            for step in range(outer):
                next_copy(part, step).wait_send()

        @pl.when(first_slab)
        def _():
            relay_copy(part, me).wait_send()

        row_copy(part).wait_send()
        for step in range(2, outer):
            relay_copy(part, row_peer(step)).wait_send()
        return carry

    lax.fori_loop(0, parts, drain, 0)
    for front in range(fronts):
        store_trace(front).wait()
        store_inner(front).wait()


def local(slabs, blocks, incident, green_interior, green_next, sources):
    fronts, rows, columns = incident.shape
    parts, half_rows = HALVES * fronts, rows // HALVES
    inner_rows = green_interior.shape[2]
    depth = green_next.shape[3]
    outer = blocks // INNER
    in_hbm = pl.BlockSpec(memory_space=pltpu.HBM)
    incident = pltpu.with_memory_space_constraint(incident, pltpu.HBM)
    sources = pltpu.with_memory_space_constraint(sources, pltpu.HBM)
    anywhere = pl.BlockSpec(memory_space=pl.ANY)
    return pl.pallas_call(
        functools.partial(kernel, slabs, blocks),
        out_shape=(
            jax.ShapeDtypeStruct((1, fronts, inner_rows, columns), jnp.float32),
            jax.ShapeDtypeStruct((1, fronts, rows, columns), jnp.float32),
        ),
        in_specs=[in_hbm] * 4,
        out_specs=(anywhere, anywhere),
        scratch_shapes=[
            pltpu.VMEM((parts, blocks, half_rows, columns), jnp.bfloat16),
            pltpu.VMEM((parts, half_rows, columns), jnp.bfloat16),
            pltpu.VMEM((parts, half_rows, columns), jnp.bfloat16),
            pltpu.VMEM((2, rows, depth), jnp.bfloat16),
            pltpu.VMEM((2, inner_rows, depth), jnp.bfloat16),
            pltpu.VMEM((fronts, rows, columns), jnp.float32),
            pltpu.VMEM((fronts, rows, columns), jnp.float32),
            pltpu.VMEM((parts, rows, columns), jnp.float32),
            pltpu.VMEM((HALVES, rows, columns), jnp.float32),
            pltpu.VMEM((2 * rows, columns), jnp.float32),
            pltpu.VMEM((2 * inner_rows, group_of(fronts) * columns), jnp.float32),
            pltpu.VMEM((fronts, rows, columns), jnp.float32),
            pltpu.VMEM((fronts, inner_rows, columns), jnp.float32),
            pltpu.SemaphoreType.DMA((parts, blocks)),
            pltpu.SemaphoreType.DMA((parts, outer)),
            pltpu.SemaphoreType.DMA((parts, outer + 1)),
            pltpu.SemaphoreType.DMA((parts, outer)),
            pltpu.SemaphoreType.DMA((3 + fronts,)),
            pltpu.SemaphoreType.DMA((2, fronts)),
        ],
        compiler_params=pltpu.CompilerParams(
            collective_id=0, has_side_effects=True, vmem_limit_bytes=VMEM_LIMIT
        ),
    )(incident, green_interior, green_next, sources)


def solution(mesh):
    return jax.shard_map(
        functools.partial(local, mesh.shape["slab"], mesh.shape["trace"]),
        mesh=mesh,
        in_specs=(
            P(None, "trace", None),
            P("slab", None, "trace", None),
            P("slab", None, "trace", None),
            P("slab", None, "trace", None),
        ),
        out_specs=(P("slab", None, "trace", None), P("slab", None, "trace", None)),
        check_vma=False,
    )
```

```python
import functools

import jax
import jax.numpy as jnp
from jax import lax
from jax.experimental import pallas as pl
from jax.experimental.pallas import tpu as pltpu
from jax.sharding import PartitionSpec as P

MESH = pl.DeviceIdType.MESH
INNER = 2
HALVES = 2
EARLY = 2
OWN = 4
VMEM_LIMIT = 48 * 1024 * 1024


def chunk_count(blocks, rows):
    count = 4
    while count > 1 and (blocks % (count * INNER) or (blocks // count * rows) % 128):
        count //= 2
    return count


def flip(value, mask):
    result = value
    bit = 1
    while bit <= mask:
        if mask & bit:
            result = result + bit - 2 * bit * lax.rem(result // bit, 2)
        bit *= 2
    return result


def visit_order(count):
    return [0] + list(range(count - 1, 0, -1))


def compute_order(count):
    return [0, 1][:count] + list(range(count - 1, 1, -1))


def group_of(fronts):
    return 2 if fronts % 2 == 0 else 1


def lanes(shape):
    return lax.broadcasted_iota(jnp.int32, shape, len(shape) - 1)


def turn(value, lead):
    columns = value.shape[-1]
    return pltpu.roll(value, (columns - lead) % columns, len(value.shape) - 1)


def split(value):
    quarter = value.shape[1] // 4
    lower = lanes(value.shape) < quarter
    near, far = turn(value, quarter), turn(value, 2 * quarter)
    return jnp.where(lower, value, near), jnp.where(lower, near, far)


def merge(first, second):
    quarter = first.shape[1] // 4
    lane = lanes(first.shape)
    low = jnp.where(lane < quarter, first, turn(second, -quarter))
    high = jnp.where(lane < 3 * quarter, turn(first, -quarter), turn(second, -2 * quarter))
    return jnp.where(lane < 2 * quarter, low, high)


def pack(value):
    rows, columns = value.shape
    lower, upper = value[: rows // 2], value[rows // 2 :]
    half = columns // 2
    return jnp.where(lanes(lower.shape) < half, lower, turn(upper, half)).astype(jnp.bfloat16)


def swap(packed):
    return pltpu.roll(packed, packed.shape[-1] // 2, len(packed.shape) - 1)


def rotate(first, second):
    quarter = first.shape[1] // 4
    real = lax.rem(lanes(first.shape) // quarter, 2) == 0
    return first + jnp.where(real, -turn(second, quarter), turn(second, -quarter))


def ordered(value):
    quarter = value.shape[1] // 4
    place = lanes(value.shape) // quarter
    return jnp.where(
        place == 1, turn(value, quarter), jnp.where(place == 2, turn(value, -quarter), value)
    )


def kernel(
    slabs,
    blocks,
    incident,
    green_interior,
    green_next,
    sources,
    interior,
    traces,
    entering,
    leaving,
    first_out,
    next_op,
    inner_op,
    incoming,
    own_sources,
    half_sources,
    half_out,
    next_sum,
    inner_sum,
    trace_out,
    inner_out,
    recv_sem,
    first_sem,
    direct_sem,
    relay_sem,
    load_sem,
    store_sem,
):
    parts, _, half_rows, columns = entering.shape
    fronts, rows = incoming.shape[:2]
    group = group_of(fronts)
    inner_rows = inner_op.shape[1]
    depth = next_op.shape[2]
    outer = blocks // INNER
    chunks = chunk_count(blocks, rows)
    per_chunk = blocks // chunks
    width = depth // chunks
    early = min(EARLY, parts)
    slab = lax.axis_index("slab")
    me = lax.axis_index("trace")
    lane_pos = lax.rem(me, INNER)
    my_outer = me // INNER
    partner = me + 1 - 2 * lane_pos
    first_slab = slab == 0
    second_slab = slab == 1
    last_slab = slab == slabs - 1
    my_chunk = me // per_chunk

    def load_incident(front):
        return pltpu.make_async_copy(
            incident.at[front], incoming.at[front], load_sem.at[3 + front]
        )

    load_next = pltpu.make_async_copy(green_next.at[0], next_op, load_sem.at[0])
    load_sources = pltpu.make_async_copy(sources.at[0], own_sources, load_sem.at[1])
    load_inner = pltpu.make_async_copy(green_interior.at[0], inner_op, load_sem.at[2])

    for front in range(fronts):
        load_incident(front).start()
    load_sources.start()
    load_next.start()
    load_inner.start()

    barrier = pltpu.get_barrier_semaphore()

    def greet(target_slab, target):
        pl.semaphore_signal(
            barrier, inc=1, device_id={"slab": target_slab, "trace": target}, device_id_type=MESH
        )

    def row_peer(step):
        return flip(my_outer, step) * INNER + lane_pos

    greet(slab, partner)
    greet(slab, row_peer(1))

    @pl.when(first_slab)
    def _():
        for step in range(1, outer):
            greet(1, row_peer(step))
            greet(slabs - 1, row_peer(step))

    @pl.when(jnp.logical_not(first_slab))
    def _():
        greet(slab - 1, partner)
        for step in range(outer):
            greet(slab - 1, row_peer(step))

    peers = 2 + jnp.where(last_slab, outer - 1, outer + 1) + jnp.where(second_slab, outer - 1, 0)
    pl.semaphore_wait(barrier, peers)

    def first_copy(part, step):
        return pltpu.make_async_remote_copy(
            src_ref=first_out.at[part],
            dst_ref=entering.at[part, me],
            send_sem=first_sem.at[part, step],
            recv_sem=recv_sem.at[part, me],
            device_id={"slab": 0, "trace": row_peer(step)},
            device_id_type=MESH,
        )

    def next_copy(part, step):
        return pltpu.make_async_remote_copy(
            src_ref=leaving.at[part],
            dst_ref=entering.at[part, me],
            send_sem=direct_sem.at[part, step],
            recv_sem=recv_sem.at[part, me],
            device_id={"slab": slab + 1, "trace": row_peer(step)},
            device_id_type=MESH,
        )

    def side_copy(part):
        return pltpu.make_async_remote_copy(
            src_ref=leaving.at[part],
            dst_ref=entering.at[part, me],
            send_sem=direct_sem.at[part, outer],
            recv_sem=recv_sem.at[part, me],
            device_id={"slab": slab + 1, "trace": partner},
            device_id_type=MESH,
        )

    def row_copy(part):
        return pltpu.make_async_remote_copy(
            src_ref=entering.at[part, partner],
            dst_ref=entering.at[part, partner],
            send_sem=relay_sem.at[part, flip(my_outer, 1)],
            recv_sem=recv_sem.at[part, partner],
            device_id={"slab": slab, "trace": row_peer(1)},
            device_id_type=MESH,
        )

    def relay_copy(part, block):
        return pltpu.make_async_remote_copy(
            src_ref=entering.at[part, block],
            dst_ref=entering.at[part, block],
            send_sem=relay_sem.at[part, block // INNER],
            recv_sem=recv_sem.at[part, block],
            device_id={"slab": slab, "trace": partner},
            device_id_type=MESH,
        )

    def store_trace(front):
        return pltpu.make_async_copy(
            trace_out.at[front], traces.at[0, front], store_sem.at[0, front]
        )

    def store_inner(front):
        return pltpu.make_async_copy(
            inner_out.at[front], interior.at[0, front], store_sem.at[1, front]
        )

    for front in range(fronts):
        load_incident(front).wait()

    @pl.when(first_slab)
    def _():
        for front in range(fronts):
            for index, value in enumerate(split(incoming[front])):
                entering[HALVES * front + index, me] = pack(value)

    def send_first(start, stop):
        for part in range(start, stop):
            first_out[part] = pack(split(incoming[part // HALVES])[part % HALVES])
            for step in visit_order(outer)[1:]:
                first_copy(part, step).start()

    @pl.when(second_slab)
    def _():
        send_first(0, early)

    @pl.when(last_slab)
    def _():
        send_first(early, parts)

    def steps_of(place):
        span = per_chunk // INNER
        return range(place * span, (place + 1) * span)

    def relay_chunk(part, order):
        for step in steps_of(visit_order(chunks)[order]):
            if step == 0:

                @pl.when(first_slab & (part + OWN < parts))
                def _():
                    relay_copy(part + OWN, me).start()

                relay_copy(part, partner).wait_recv()
                row_copy(part).start()
            elif step > 1:
                relay_copy(part, row_peer(step)).wait_recv()
                relay_copy(part, row_peer(step)).start()

    def await_chunk(part, place):
        for step in steps_of(place):
            mine = row_peer(step)
            other = mine + 1 - 2 * lane_pos
            if step == 0:

                @pl.when(jnp.logical_not(first_slab))
                def _():
                    relay_copy(part, mine).wait_recv()

            else:
                if step == 1:
                    relay_copy(part, mine).wait_recv()
                relay_copy(part, other).wait_recv()

    def packed_rows(part, chunk):
        return entering[part, pl.ds(chunk * per_chunk, per_chunk)]

    def stacked(lower, upper):
        return jnp.concatenate([lower, upper], axis=1).reshape(width, columns)

    def matrix_of(op, chunk):
        start = pl.multiple_of(chunk * width, width)
        return op[:, :, pl.ds(start, width)].reshape(2 * op.shape[1], width)

    def next_chunk(part, place):
        chunk = flip(my_chunk, place)
        value = packed_rows(part, chunk)
        product = jnp.dot(
            matrix_of(next_op, chunk),
            stacked(value, swap(value)),
            preferred_element_type=jnp.float32,
        )
        if place == 0:
            next_sum[...] = product
        else:
            next_sum[...] += product

    def inner_chunk(front, chunk, fresh):
        both = []
        for index in range(group):
            low = packed_rows(HALVES * (front + index), chunk)
            high = packed_rows(HALVES * (front + index) + 1, chunk)
            lower = lanes(low.shape) < columns // 2
            both.append(
                stacked(jnp.where(lower, low, swap(high)), jnp.where(lower, swap(low), high))
            )
        product = jnp.dot(
            matrix_of(inner_op, chunk),
            jnp.concatenate(both, axis=1),
            preferred_element_type=jnp.float32,
        )
        if fresh:
            inner_sum[...] = product
        else:
            inner_sum[...] += product

    def inner_finish(front):
        for index in range(group):
            place = pl.ds(index * columns, columns)
            result = rotate(inner_sum[0:inner_rows, place], inner_sum[inner_rows:, place])
            inner_out[front + index] = ordered(result)
            store_inner(front + index).start()

    def inner_group(front):
        inner_chunk(front, 0, True)

        def more(chunk, carry):
            inner_chunk(front, chunk, False)
            return carry

        lax.fori_loop(1, chunks, more, 0)
        inner_finish(front)

    def relay_ahead(part, order):
        for lead, mine in leads:
            step, later = divmod(order + lead, chunks)

            @pl.when(mine & (part + step < parts))
            def _():
                relay_chunk(part + step, later)

    @pl.when(first_slab)
    def _():
        for part in range(min(OWN, parts)):
            relay_copy(part, me).start()

    leads = [(6, first_slab), (4, jnp.logical_not(first_slab))]
    for lead, mine in leads:

        @pl.when(mine)
        def _():
            for count in range(lead):
                relay_chunk(count // chunks, count % chunks)

    load_sources.wait()
    for front in range(fronts):
        for index, value in enumerate(split(own_sources[front])):
            half_sources[HALVES * front + index] = value
    load_next.wait()
    load_inner.wait()

    def one_part(part, carry):
        closing = part == parts - 1
        side = lax.rem(part, HALVES)
        front = part // HALVES
        for order, place in enumerate(compute_order(chunks)):
            await_chunk(part, place)
            next_chunk(part, place)

            @pl.when(closing & last_slab)
            def _():
                inner_chunk(fronts - group, flip(my_chunk, place), order == 0)

            relay_ahead(part, order)

        result = rotate(next_sum[0:rows], next_sum[rows:]) + half_sources[part]
        leaving[part] = pack(result)

        @pl.when(jnp.logical_not(last_slab))
        def _():
            next_copy(part, 0).start()
            side_copy(part).start()
            for step in visit_order(outer)[1:]:
                next_copy(part, step).start()

        half_out[side] = result

        @pl.when(side == HALVES - 1)
        def _():
            trace_out[front] = merge(half_out[0], half_out[1])
            store_trace(front).start()

        full = lax.rem(part, group * HALVES) == group * HALVES - 1

        @pl.when(full & last_slab & jnp.logical_not(closing))
        def _():
            inner_group(front + 1 - group)

        return carry

    lax.fori_loop(0, parts, one_part, 0)

    @pl.when(last_slab)
    def _():
        inner_finish(fronts - group)

    @pl.when(jnp.logical_not(last_slab))
    def _():
        def rest(index, carry):
            inner_group(index * group)
            return carry

        lax.fori_loop(0, fronts // group, rest, 0)

    def drain_first(start, stop):
        for part in range(start, stop):
            for step in range(1, outer):
                first_copy(part, step).wait_send()

    @pl.when(second_slab)
    def _():
        drain_first(0, early)

    @pl.when(last_slab)
    def _():
        drain_first(early, parts)

    def drain(part, carry):
        @pl.when(jnp.logical_not(last_slab))
        def _():
            side_copy(part).wait_send()
            for step in range(outer):
                next_copy(part, step).wait_send()

        @pl.when(first_slab)
        def _():
            relay_copy(part, me).wait_send()

        row_copy(part).wait_send()
        for step in range(2, outer):
            relay_copy(part, row_peer(step)).wait_send()
        return carry

    lax.fori_loop(0, parts, drain, 0)
    for front in range(fronts):
        store_trace(front).wait()
        store_inner(front).wait()


def deliver(interior, traces, interior_out, traces_out, sem):
    copies = []
    for front in range(traces.shape[1]):
        copies.append((interior.at[0, front], interior_out.at[0, front], sem.at[0, front]))
        copies.append((traces.at[0, front], traces_out.at[0, front], sem.at[1, front]))
    for copy in copies:
        pltpu.make_async_copy(*copy).start()
    for copy in copies:
        pltpu.make_async_copy(*copy).wait()


def local(slabs, blocks, incident, green_interior, green_next, sources):
    fronts, rows, columns = incident.shape
    parts, half_rows = HALVES * fronts, rows // HALVES
    inner_rows = green_interior.shape[2]
    depth = green_next.shape[3]
    outer = blocks // INNER
    in_hbm = pl.BlockSpec(memory_space=pltpu.HBM)
    incident = pltpu.with_memory_space_constraint(incident, pltpu.HBM)
    sources = pltpu.with_memory_space_constraint(sources, pltpu.HBM)
    anywhere = pl.BlockSpec(memory_space=pl.ANY)
    shapes = (
        jax.ShapeDtypeStruct((1, fronts, inner_rows, columns), jnp.float32),
        jax.ShapeDtypeStruct((1, fronts, rows, columns), jnp.float32),
    )
    results = pl.pallas_call(
        functools.partial(kernel, slabs, blocks),
        out_shape=shapes,
        in_specs=[in_hbm] * 4,
        out_specs=(anywhere, anywhere),
        scratch_shapes=[
            pltpu.VMEM((parts, blocks, half_rows, columns), jnp.bfloat16),
            pltpu.VMEM((parts, half_rows, columns), jnp.bfloat16),
            pltpu.VMEM((parts, half_rows, columns), jnp.bfloat16),
            pltpu.VMEM((2, rows, depth), jnp.bfloat16),
            pltpu.VMEM((2, inner_rows, depth), jnp.bfloat16),
            pltpu.VMEM((fronts, rows, columns), jnp.float32),
            pltpu.VMEM((fronts, rows, columns), jnp.float32),
            pltpu.VMEM((parts, rows, columns), jnp.float32),
            pltpu.VMEM((HALVES, rows, columns), jnp.float32),
            pltpu.VMEM((2 * rows, columns), jnp.float32),
            pltpu.VMEM((2 * inner_rows, group_of(fronts) * columns), jnp.float32),
            pltpu.VMEM((fronts, rows, columns), jnp.float32),
            pltpu.VMEM((fronts, inner_rows, columns), jnp.float32),
            pltpu.SemaphoreType.DMA((parts, blocks)),
            pltpu.SemaphoreType.DMA((parts, outer)),
            pltpu.SemaphoreType.DMA((parts, outer + 1)),
            pltpu.SemaphoreType.DMA((parts, outer)),
            pltpu.SemaphoreType.DMA((3 + fronts,)),
            pltpu.SemaphoreType.DMA((2, fronts)),
        ],
        compiler_params=pltpu.CompilerParams(
            collective_id=0, has_side_effects=True, vmem_limit_bytes=VMEM_LIMIT
        ),
    )(incident, green_interior, green_next, sources)
    return pl.pallas_call(
        deliver,
        out_shape=shapes,
        in_specs=[anywhere] * 2,
        out_specs=(in_hbm, in_hbm),
        scratch_shapes=[pltpu.SemaphoreType.DMA((2, fronts))],
        compiler_params=pltpu.CompilerParams(vmem_limit_bytes=1024 * 1024),
    )(*results)


def solution(mesh):
    return jax.shard_map(
        functools.partial(local, mesh.shape["slab"], mesh.shape["trace"]),
        mesh=mesh,
        in_specs=(
            P(None, "trace", None),
            P("slab", None, "trace", None),
            P("slab", None, "trace", None),
            P("slab", None, "trace", None),
        ),
        out_specs=(P("slab", None, "trace", None), P("slab", None, "trace", None)),
        check_vma=False,
    )
```

```python
import functools

import jax
import jax.numpy as jnp
from jax import lax
from jax.experimental import pallas as pl
from jax.experimental.pallas import tpu as pltpu
from jax.sharding import PartitionSpec as P

MESH = pl.DeviceIdType.MESH
INNER = 2
HALVES = 2
EARLY = 2
OWN = 4
VMEM_LIMIT = 48 * 1024 * 1024


def chunk_count(blocks, rows):
    count = 4
    while count > 1 and (blocks % (count * INNER) or (blocks // count * rows) % 128):
        count //= 2
    return count


def flip(value, mask):
    result = value
    bit = 1
    while bit <= mask:
        if mask & bit:
            result = result + bit - 2 * bit * lax.rem(result // bit, 2)
        bit *= 2
    return result


def visit_order(count):
    return [0] + list(range(count - 1, 0, -1))


def compute_order(count):
    return [0, 1][:count] + list(range(count - 1, 1, -1))


def group_of(fronts):
    return 2 if fronts % 2 == 0 else 1


def lanes(shape):
    return lax.broadcasted_iota(jnp.int32, shape, len(shape) - 1)


def turn(value, lead):
    columns = value.shape[-1]
    return pltpu.roll(value, (columns - lead) % columns, len(value.shape) - 1)


def split(value):
    quarter = value.shape[1] // 4
    lower = lanes(value.shape) < quarter
    near, far = turn(value, quarter), turn(value, 2 * quarter)
    return jnp.where(lower, value, near), jnp.where(lower, near, far)


def merge(first, second):
    quarter = first.shape[1] // 4
    lane = lanes(first.shape)
    low = jnp.where(lane < quarter, first, turn(second, -quarter))
    high = jnp.where(lane < 3 * quarter, turn(first, -quarter), turn(second, -2 * quarter))
    return jnp.where(lane < 2 * quarter, low, high)


def pack(value):
    rows, columns = value.shape
    lower, upper = value[: rows // 2], value[rows // 2 :]
    half = columns // 2
    return jnp.where(lanes(lower.shape) < half, lower, turn(upper, half)).astype(jnp.bfloat16)


def swap(packed):
    return pltpu.roll(packed, packed.shape[-1] // 2, len(packed.shape) - 1)


def rotate(first, second):
    quarter = first.shape[1] // 4
    real = lax.rem(lanes(first.shape) // quarter, 2) == 0
    return first + jnp.where(real, -turn(second, quarter), turn(second, -quarter))


def ordered(value):
    quarter = value.shape[1] // 4
    place = lanes(value.shape) // quarter
    return jnp.where(
        place == 1, turn(value, quarter), jnp.where(place == 2, turn(value, -quarter), value)
    )


def kernel(
    slabs,
    blocks,
    incident,
    green_interior,
    green_next,
    sources,
    interior,
    traces,
    entering,
    leaving,
    first_out,
    next_op,
    inner_op,
    incoming,
    own_sources,
    half_sources,
    half_out,
    next_sum,
    inner_sum,
    trace_out,
    inner_out,
    recv_sem,
    first_sem,
    direct_sem,
    relay_sem,
    load_sem,
    store_sem,
):
    parts, _, half_rows, columns = entering.shape
    fronts, rows = incoming.shape[:2]
    group = group_of(fronts)
    inner_rows = inner_op.shape[1]
    depth = next_op.shape[2]
    outer = blocks // INNER
    chunks = chunk_count(blocks, rows)
    per_chunk = blocks // chunks
    width = depth // chunks
    early = min(EARLY, parts)
    slab = lax.axis_index("slab")
    me = lax.axis_index("trace")
    lane_pos = lax.rem(me, INNER)
    my_outer = me // INNER
    partner = me + 1 - 2 * lane_pos
    first_slab = slab == 0
    second_slab = slab == 1
    last_slab = slab == slabs - 1
    my_chunk = me // per_chunk

    def load_incident(front):
        return pltpu.make_async_copy(
            incident.at[front], incoming.at[front], load_sem.at[3 + front]
        )

    load_next = pltpu.make_async_copy(green_next.at[0], next_op, load_sem.at[0])
    load_sources = pltpu.make_async_copy(sources.at[0], own_sources, load_sem.at[1])
    load_inner = pltpu.make_async_copy(green_interior.at[0], inner_op, load_sem.at[2])

    for front in range(fronts):
        load_incident(front).start()
    load_sources.start()
    load_next.start()
    load_inner.start()

    barrier = pltpu.get_barrier_semaphore()

    def greet(target_slab, target):
        pl.semaphore_signal(
            barrier, inc=1, device_id={"slab": target_slab, "trace": target}, device_id_type=MESH
        )

    def row_peer(step):
        return flip(my_outer, step) * INNER + lane_pos

    greet(slab, partner)
    greet(slab, row_peer(1))

    @pl.when(first_slab)
    def _():
        for step in range(1, outer):
            greet(1, row_peer(step))
            greet(slabs - 1, row_peer(step))

    @pl.when(jnp.logical_not(first_slab))
    def _():
        greet(slab - 1, partner)
        for step in range(outer):
            greet(slab - 1, row_peer(step))

    peers = 2 + jnp.where(last_slab, outer - 1, outer + 1) + jnp.where(second_slab, outer - 1, 0)
    pl.semaphore_wait(barrier, peers)

    def first_copy(part, step):
        return pltpu.make_async_remote_copy(
            src_ref=first_out.at[part],
            dst_ref=entering.at[part, me],
            send_sem=first_sem.at[part, step],
            recv_sem=recv_sem.at[part, me],
            device_id={"slab": 0, "trace": row_peer(step)},
            device_id_type=MESH,
        )

    def next_copy(part, step):
        return pltpu.make_async_remote_copy(
            src_ref=leaving.at[part],
            dst_ref=entering.at[part, me],
            send_sem=direct_sem.at[part, step],
            recv_sem=recv_sem.at[part, me],
            device_id={"slab": slab + 1, "trace": row_peer(step)},
            device_id_type=MESH,
        )

    def side_copy(part):
        return pltpu.make_async_remote_copy(
            src_ref=leaving.at[part],
            dst_ref=entering.at[part, me],
            send_sem=direct_sem.at[part, outer],
            recv_sem=recv_sem.at[part, me],
            device_id={"slab": slab + 1, "trace": partner},
            device_id_type=MESH,
        )

    def row_copy(part):
        return pltpu.make_async_remote_copy(
            src_ref=entering.at[part, partner],
            dst_ref=entering.at[part, partner],
            send_sem=relay_sem.at[part, flip(my_outer, 1)],
            recv_sem=recv_sem.at[part, partner],
            device_id={"slab": slab, "trace": row_peer(1)},
            device_id_type=MESH,
        )

    def relay_copy(part, block):
        return pltpu.make_async_remote_copy(
            src_ref=entering.at[part, block],
            dst_ref=entering.at[part, block],
            send_sem=relay_sem.at[part, block // INNER],
            recv_sem=recv_sem.at[part, block],
            device_id={"slab": slab, "trace": partner},
            device_id_type=MESH,
        )

    def store_trace(front):
        return pltpu.make_async_copy(
            trace_out.at[front], traces.at[0, front], store_sem.at[0, front]
        )

    def store_inner(front):
        return pltpu.make_async_copy(
            inner_out.at[front], interior.at[0, front], store_sem.at[1, front]
        )

    for front in range(fronts):
        load_incident(front).wait()

    @pl.when(first_slab)
    def _():
        for front in range(fronts):
            for index, value in enumerate(split(incoming[front])):
                entering[HALVES * front + index, me] = pack(value)

    def send_first(start, stop):
        for part in range(start, stop):
            first_out[part] = pack(split(incoming[part // HALVES])[part % HALVES])
            for step in visit_order(outer)[1:]:
                first_copy(part, step).start()

    @pl.when(second_slab)
    def _():
        send_first(0, early)

    @pl.when(last_slab)
    def _():
        send_first(early, parts)

    def steps_of(place):
        span = per_chunk // INNER
        return range(place * span, (place + 1) * span)

    def relay_chunk(part, order):
        for step in steps_of(visit_order(chunks)[order]):
            if step == 0:

                @pl.when(first_slab & (part + OWN < parts))
                def _():
                    relay_copy(part + OWN, me).start()

                relay_copy(part, partner).wait_recv()
                row_copy(part).start()
            elif step > 1:
                relay_copy(part, row_peer(step)).wait_recv()
                relay_copy(part, row_peer(step)).start()

    def await_chunk(part, place):
        for step in steps_of(place):
            mine = row_peer(step)
            other = mine + 1 - 2 * lane_pos
            if step == 0:

                @pl.when(jnp.logical_not(first_slab))
                def _():
                    relay_copy(part, mine).wait_recv()

            else:
                if step == 1:
                    relay_copy(part, mine).wait_recv()
                relay_copy(part, other).wait_recv()

    def packed_rows(part, chunk):
        return entering[part, pl.ds(chunk * per_chunk, per_chunk)]

    def stacked(lower, upper):
        return jnp.concatenate([lower, upper], axis=1).reshape(width, columns)

    def matrix_of(op, chunk):
        start = pl.multiple_of(chunk * width, width)
        return op[:, :, pl.ds(start, width)].reshape(2 * op.shape[1], width)

    def next_chunk(part, place):
        chunk = flip(my_chunk, place)
        value = packed_rows(part, chunk)
        product = jnp.dot(
            matrix_of(next_op, chunk),
            stacked(value, swap(value)),
            preferred_element_type=jnp.float32,
        )
        if place == 0:
            next_sum[...] = product
        else:
            next_sum[...] += product

    def inner_chunk(front, chunk, fresh):
        both = []
        for index in range(group):
            low = packed_rows(HALVES * (front + index), chunk)
            high = packed_rows(HALVES * (front + index) + 1, chunk)
            lower = lanes(low.shape) < columns // 2
            both.append(
                stacked(jnp.where(lower, low, swap(high)), jnp.where(lower, swap(low), high))
            )
        product = jnp.dot(
            matrix_of(inner_op, chunk),
            jnp.concatenate(both, axis=1),
            preferred_element_type=jnp.float32,
        )
        if fresh:
            inner_sum[...] = product
        else:
            inner_sum[...] += product

    def inner_finish(front):
        for index in range(group):
            place = pl.ds(index * columns, columns)
            result = rotate(inner_sum[0:inner_rows, place], inner_sum[inner_rows:, place])
            inner_out[front + index] = ordered(result)
            store_inner(front + index).start()

    def inner_group(front):
        inner_chunk(front, 0, True)

        def more(chunk, carry):
            inner_chunk(front, chunk, False)
            return carry

        lax.fori_loop(1, chunks, more, 0)
        inner_finish(front)

    def relay_ahead(part, order):
        for lead, mine in leads:
            step, later = divmod(order + lead, chunks)

            @pl.when(mine & (part + step < parts))
            def _():
                relay_chunk(part + step, later)

    @pl.when(first_slab)
    def _():
        for part in range(min(OWN, parts)):
            relay_copy(part, me).start()

    leads = [(6, first_slab), (4, jnp.logical_not(first_slab))]
    for lead, mine in leads:

        @pl.when(mine)
        def _():
            for count in range(lead):
                relay_chunk(count // chunks, count % chunks)

    load_sources.wait()
    for front in range(fronts):
        for index, value in enumerate(split(own_sources[front])):
            half_sources[HALVES * front + index] = value
    load_next.wait()
    load_inner.wait()

    def one_part(part, carry):
        closing = part == parts - 1
        side = lax.rem(part, HALVES)
        front = part // HALVES
        for order, place in enumerate(compute_order(chunks)):
            await_chunk(part, place)
            next_chunk(part, place)

            @pl.when(closing & last_slab)
            def _():
                inner_chunk(fronts - group, flip(my_chunk, place), order == 0)

            relay_ahead(part, order)

        result = rotate(next_sum[0:rows], next_sum[rows:]) + half_sources[part]
        leaving[part] = pack(result)

        @pl.when(jnp.logical_not(last_slab))
        def _():
            next_copy(part, 0).start()
            side_copy(part).start()
            for step in visit_order(outer)[1:]:
                next_copy(part, step).start()

        half_out[side] = result

        @pl.when(side == HALVES - 1)
        def _():
            trace_out[front] = merge(half_out[0], half_out[1])
            store_trace(front).start()

        place = lax.rem(part, group * HALVES)
        prior = (part // (group * HALVES) - 1) * group
        middle = (chunks + 1) // 2
        if group > 1:

            @pl.when(last_slab & (prior >= 0) & (place == 0))
            def _():
                for chunk in range(middle):
                    inner_chunk(prior, chunk, chunk == 0)

            @pl.when(last_slab & (prior >= 0) & (place == 1))
            def _():
                for chunk in range(middle, chunks):
                    inner_chunk(prior, chunk, False)
                inner_finish(prior)

        else:

            @pl.when(last_slab & jnp.logical_not(closing) & (place == HALVES - 1))
            def _():
                inner_group(front)

        return carry

    lax.fori_loop(0, parts, one_part, 0)

    @pl.when(last_slab)
    def _():
        inner_finish(fronts - group)

    @pl.when(jnp.logical_not(last_slab))
    def _():
        def rest(index, carry):
            inner_group(index * group)
            return carry

        lax.fori_loop(0, fronts // group, rest, 0)

    def drain_first(start, stop):
        for part in range(start, stop):
            for step in range(1, outer):
                first_copy(part, step).wait_send()

    @pl.when(second_slab)
    def _():
        drain_first(0, early)

    @pl.when(last_slab)
    def _():
        drain_first(early, parts)

    def drain(part, carry):
        @pl.when(jnp.logical_not(last_slab))
        def _():
            side_copy(part).wait_send()
            for step in range(outer):
                next_copy(part, step).wait_send()

        @pl.when(first_slab)
        def _():
            relay_copy(part, me).wait_send()

        row_copy(part).wait_send()
        for step in range(2, outer):
            relay_copy(part, row_peer(step)).wait_send()
        return carry

    lax.fori_loop(0, parts, drain, 0)
    for front in range(fronts):
        store_trace(front).wait()
        store_inner(front).wait()


def deliver(interior, traces, interior_out, traces_out, sem):
    copies = []
    for front in range(traces.shape[1]):
        copies.append((interior.at[0, front], interior_out.at[0, front], sem.at[0, front]))
        copies.append((traces.at[0, front], traces_out.at[0, front], sem.at[1, front]))
    for copy in copies:
        pltpu.make_async_copy(*copy).start()
    for copy in copies:
        pltpu.make_async_copy(*copy).wait()


def local(slabs, blocks, incident, green_interior, green_next, sources):
    fronts, rows, columns = incident.shape
    parts, half_rows = HALVES * fronts, rows // HALVES
    inner_rows = green_interior.shape[2]
    depth = green_next.shape[3]
    outer = blocks // INNER
    in_hbm = pl.BlockSpec(memory_space=pltpu.HBM)
    incident = pltpu.with_memory_space_constraint(incident, pltpu.HBM)
    sources = pltpu.with_memory_space_constraint(sources, pltpu.HBM)
    anywhere = pl.BlockSpec(memory_space=pl.ANY)
    shapes = (
        jax.ShapeDtypeStruct((1, fronts, inner_rows, columns), jnp.float32),
        jax.ShapeDtypeStruct((1, fronts, rows, columns), jnp.float32),
    )
    results = pl.pallas_call(
        functools.partial(kernel, slabs, blocks),
        out_shape=shapes,
        in_specs=[in_hbm] * 4,
        out_specs=(anywhere, anywhere),
        scratch_shapes=[
            pltpu.VMEM((parts, blocks, half_rows, columns), jnp.bfloat16),
            pltpu.VMEM((parts, half_rows, columns), jnp.bfloat16),
            pltpu.VMEM((parts, half_rows, columns), jnp.bfloat16),
            pltpu.VMEM((2, rows, depth), jnp.bfloat16),
            pltpu.VMEM((2, inner_rows, depth), jnp.bfloat16),
            pltpu.VMEM((fronts, rows, columns), jnp.float32),
            pltpu.VMEM((fronts, rows, columns), jnp.float32),
            pltpu.VMEM((parts, rows, columns), jnp.float32),
            pltpu.VMEM((HALVES, rows, columns), jnp.float32),
            pltpu.VMEM((2 * rows, columns), jnp.float32),
            pltpu.VMEM((2 * inner_rows, group_of(fronts) * columns), jnp.float32),
            pltpu.VMEM((fronts, rows, columns), jnp.float32),
            pltpu.VMEM((fronts, inner_rows, columns), jnp.float32),
            pltpu.SemaphoreType.DMA((parts, blocks)),
            pltpu.SemaphoreType.DMA((parts, outer)),
            pltpu.SemaphoreType.DMA((parts, outer + 1)),
            pltpu.SemaphoreType.DMA((parts, outer)),
            pltpu.SemaphoreType.DMA((3 + fronts,)),
            pltpu.SemaphoreType.DMA((2, fronts)),
        ],
        compiler_params=pltpu.CompilerParams(
            collective_id=0, has_side_effects=True, vmem_limit_bytes=VMEM_LIMIT
        ),
    )(incident, green_interior, green_next, sources)
    return pl.pallas_call(
        deliver,
        out_shape=shapes,
        in_specs=[anywhere] * 2,
        out_specs=(in_hbm, in_hbm),
        scratch_shapes=[pltpu.SemaphoreType.DMA((2, fronts))],
        compiler_params=pltpu.CompilerParams(vmem_limit_bytes=1024 * 1024),
    )(*results)


def solution(mesh):
    return jax.shard_map(
        functools.partial(local, mesh.shape["slab"], mesh.shape["trace"]),
        mesh=mesh,
        in_specs=(
            P(None, "trace", None),
            P("slab", None, "trace", None),
            P("slab", None, "trace", None),
            P("slab", None, "trace", None),
        ),
        out_specs=(P("slab", None, "trace", None), P("slab", None, "trace", None)),
        check_vma=False,
    )
```
